32 devices in a mesh: dp: 8 (over y, x, core), mp: 4 (over z).
Axes of the slice: x: 2, y: 2, z: 4, core: 2. Of those that a mesh axis runs over, the one named last changes fastest.
Arguments:
- hidden_states: bfloat16 [4096, 4096], P('dp', 'mp'), may hold values from -40 to 40
- norm_gain: float32 [1, 4096], replicated, may hold values from 0.1 to 1.9
- query_weight: bfloat16 [1, 4096, 4096], P(None, 'dp', 'mp'), may hold values from -0.01171875 to 0.01171875
- keyvalue_weight: bfloat16 [1, 4096, 2, 4096], P(None, 'dp', None, 'mp'), may hold values from -0.09375 to 0.09375
- output_weight: bfloat16 [1, 4096, 4096], P(None, 'dp', 'mp'), may hold values from -0.09375 to 0.09375
- position_bias: float32 [1, 32, 64], P(None, None, 'mp'), may hold values from -8 to 250
- lengths: int32 [32], P('dp'), may hold values from 16 to 128
Outputs:
- layer_output: bfloat16 [4096, 4096], P('dp', 'mp')
The draws below stay inside these ranges and needn't reach their ends.
All inputs are finite; a program needn't handle non-finite values.
Results may differ from the reference program's by a relative error of at most 0.006.
Values may be sent and summed in bfloat16 or wider, within the bound.
No kernel may reach another device: no remote copies, remote signals or barrier semaphores. Data moves between devices by JAX's collectives and lax.ppermute only.
A program may use at most 128 MiB of HBM per device.

```python
import jax
import jax.numpy as jnp
import numpy as np
from jax import lax

D = 4096
HEADS = 64
DH = 64
BUCKETS = 32
DIST = 128
LEN = 128
LAYERS = 1
INNER = 4096
CAPTIONS = 32
TOKENS = 4096


def draw_hidden_states(key, part):
    key_rows, key_columns, key_noise = jax.random.split(key, 3)
    row_scale = jnp.exp(jax.random.uniform(key_rows, (TOKENS, 1), jnp.float32, np.log(0.3), np.log(3.0)))
    column_scale = jnp.exp(jax.random.uniform(key_columns, (1, D), jnp.float32, np.log(0.3), np.log(3.0)))
    gaussian = jax.random.normal(key_noise, (TOKENS, D), jnp.float32)
    values = row_scale * column_scale * gaussian
    return jnp.clip(values, -40.0, 40.0).astype(jnp.bfloat16)


def draw_position_bias(key, part):
    key_base = jax.random.fold_in(key, 0)
    baseline = jnp.clip(1.5 * jax.random.normal(key_base, (LAYERS, BUCKETS, HEADS), jnp.float32), -8.0, 8.0)
    return baseline


def set_ends(drawn, stream_key, low, top_value):
    longest = drawn.shape.index(max(drawn.shape))
    spots = []
    for shift in (0, 1):
        where = [jax.random.randint(jax.random.fold_in(stream_key, axis), (), 0, length) for axis, length in enumerate(drawn.shape)]
        where[longest] = (where[longest] + shift) % drawn.shape[longest]
        spots.append(tuple(where))
    return drawn.at[spots[0]].set(low).at[spots[1]].set(top_value)


def shard_levels(own_key, shape, cuts, smallest, top_value):
    def one(position, parts):
        steps = jax.random.uniform(jax.random.fold_in(jax.random.fold_in(own_key, 6), position), (parts,), jnp.float32, smallest / len(cuts), top_value / len(cuts))
        return jnp.repeat(jnp.exp(steps), shape[position] // parts).reshape((-1,) + (1,) * (len(shape) - position - 1))

    loudness = one(*cuts[0])
    for cut in cuts[1:]:
        loudness = loudness * one(*cut)
    return loudness


def centred(stream_key, extent, spread, limit, cuts=(), kind=jnp.bfloat16):
    drawn = jax.random.normal(stream_key, extent, jnp.float32) * spread
    if len(cuts) > 0:
        drawn = shard_levels(stream_key, extent, cuts, -0.22, 0.18) * drawn
    return jnp.clip(drawn, min=-limit, max=limit).astype(kind)


def setup_inputs(seed: int = 0) -> dict:
    arg_keys = jax.random.split(jax.random.key(seed), 8)
    return {
        "hidden_states": draw_hidden_states(jax.random.fold_in(arg_keys[7], 71), 0),
        "norm_gain": jnp.clip(1.0 + 0.18 * jax.random.normal(arg_keys[1], (LAYERS, D), jnp.float32), 0.1, 1.9),
        "query_weight": centred(arg_keys[2], (LAYERS, D, INNER), (D * DH) ** -0.5, 0.01171875, ((1, 8), (2, 4))),
        "keyvalue_weight": centred(arg_keys[3], (LAYERS, D, 2, INNER), D ** -0.5, 0.09375, ((1, 8), (3, 4))),
        "output_weight": centred(arg_keys[4], (LAYERS, D, INNER), INNER ** -0.5, 0.09375, ((1, 8), (2, 4))),
        "position_bias": draw_position_bias(jax.random.fold_in(arg_keys[7], 71), 0),
        "lengths": set_ends(jax.random.randint(arg_keys[6], (CAPTIONS,), LEN // 8, LEN + 1), jax.random.fold_in(arg_keys[6], 1), LEN // 8, LEN).astype(jnp.int32),
    }


epsilon = 1e-06

def bucket_table():
    half_count = BUCKETS // 2
    exact_count = half_count // 2
    positions = np.arange(LEN)
    relative = positions[None, :] - positions[:, None]
    distance = np.abs(relative)
    scaled = np.log(np.maximum(distance, 1) / exact_count) / np.log(DIST / exact_count) * (half_count - exact_count)
    far_bucket = np.minimum(exact_count + np.floor(scaled + 1e-09).astype(np.int32), half_count - 1)
    near_bucket = np.where(distance < exact_count, distance, far_bucket)
    return (near_bucket + np.where(relative > 0, half_count, 0)).astype(np.int32)

def normed_rows(hidden, gain_row):
    values = hidden.astype(jnp.float32)
    mean_square = lax.optimization_barrier(jnp.mean(values * values, axis=-1, keepdims=True))
    return (values * lax.rsqrt(mean_square + epsilon) * gain_row).astype(jnp.bfloat16)

def reference(hidden_states, norm_gain, query_weight, keyvalue_weight, output_weight, position_bias, lengths):
    buckets = bucket_table()
    hidden = hidden_states
    for layer_index in range(LAYERS):
        normed = normed_rows(hidden, norm_gain[layer_index])
        queries = jnp.dot(normed, query_weight[layer_index], preferred_element_type=jnp.float32).astype(jnp.bfloat16)
        paired = jnp.dot(normed, keyvalue_weight[layer_index].reshape(D, 2 * INNER), preferred_element_type=jnp.float32).astype(jnp.bfloat16)
        key_rows = paired[:, :INNER].reshape(CAPTIONS, LEN, HEADS, DH)
        value_rows = paired[:, INNER:].reshape(CAPTIONS, LEN, HEADS, DH)
        position_terms = jnp.transpose(position_bias[layer_index][buckets], (2, 0, 1))

        def attend_caption(inputs):
            query_block, key_block, value_block, length = inputs
            scores = jnp.einsum('qhe,khe->hqk', query_block.astype(jnp.float32), key_block.astype(jnp.float32)) + position_terms
            visible = jnp.arange(LEN) < length
            scores = jnp.where(visible[None, None, :], scores, -1e+30)
            maxima = lax.optimization_barrier(jnp.max(scores, axis=-1, keepdims=True))
            raised = jnp.exp(scores - maxima)
            weights = (raised / lax.optimization_barrier(jnp.sum(raised, axis=-1, keepdims=True))).astype(jnp.bfloat16)
            mixture = jnp.einsum('hqk,khe->qhe', weights.astype(jnp.float32), value_block.astype(jnp.float32))
            return mixture.astype(jnp.bfloat16).reshape(LEN, INNER)
        attended = lax.map(attend_caption, (queries.reshape(CAPTIONS, LEN, HEADS, DH), key_rows, value_rows, lengths))
        attended = attended.reshape(TOKENS, INNER)
        projected = jnp.dot(attended, output_weight[layer_index].T, preferred_element_type=jnp.float32)
        hidden = (hidden.astype(jnp.float32) + projected).astype(jnp.bfloat16)
    return hidden
```

```python
import functools

import jax
import jax.numpy as jnp
import numpy as np
from jax import lax
from jax.experimental import pallas as pl
from jax.experimental.pallas import tpu as pltpu
from jax.sharding import PartitionSpec as P

DH = 64
BUCKETS = 32
DIST = 128
LEN = 128
LANES = 128

epsilon = 1e-06

ANY = pl.BlockSpec(memory_space=pl.ANY)
SMEM = pl.BlockSpec(memory_space=pltpu.SMEM)
VMEM = pl.BlockSpec(memory_space=pltpu.VMEM)


def bucket_table():
    half_count = BUCKETS // 2
    exact_count = half_count // 2
    positions = np.arange(LEN)
    relative = positions[None, :] - positions[:, None]
    distance = np.abs(relative)
    scaled = (
        np.log(np.maximum(distance, 1) / exact_count)
        / np.log(DIST / exact_count)
        * (half_count - exact_count)
    )
    far_bucket = np.minimum(exact_count + np.floor(scaled + 1e-09).astype(np.int32), half_count - 1)
    near_bucket = np.where(distance < exact_count, distance, far_bucket)
    return (near_bucket + np.where(relative > 0, half_count, 0)).astype(np.int32)


def low_bit(p):
    return p & -p


def high_bit(p):
    return 1 << (p.bit_length() - 1)


def is_power(p):
    return p & (p - 1) == 0


def norm_kernel(groups, parts, *refs):
    xs = refs[: groups * parts]
    gain_ref, out_ref = refs[groups * parts :]
    features = parts * xs[0].shape[1]
    for u in range(groups):
        total = None
        for t in range(parts):
            x = xs[u * parts + t][...].astype(jnp.float32)
            s = jnp.sum(x * x, axis=-1, keepdims=True)
            total = s if total is None else total + s
        scale = lax.rsqrt(total * (1.0 / features) + epsilon)
        for t in range(parts):
            x = xs[u * parts + t][...].astype(jnp.float32)
            out_ref[t, u] = (x * scale * gain_ref[t][None, :]).astype(jnp.bfloat16)


def norm_call(pieces, gain_parts):
    groups, parts = len(pieces), len(pieces[0])
    rows, f = pieces[0][0].shape
    step = min(rows, 128)
    flat = [pieces[u][t] for u in range(groups) for t in range(parts)]
    return pl.pallas_call(
        functools.partial(norm_kernel, groups, parts),
        grid=(rows // step,),
        in_specs=[pl.BlockSpec((step, f), lambda i: (i, 0))] * len(flat)
        + [pl.BlockSpec((parts, f), lambda i: (0, 0))],
        out_specs=pl.BlockSpec((parts, groups, step, f), lambda i: (0, 0, i, 0)),
        out_shape=jax.ShapeDtypeStruct((parts, groups, rows, f), jnp.bfloat16),
        compiler_params=pltpu.CompilerParams(vmem_limit_bytes=48 * 2**20),
        cost_estimate=pl.CostEstimate(
            flops=8 * groups * parts * rows * f,
            bytes_accessed=4 * groups * parts * rows * f,
            transcendentals=0,
        ),
        name="norm",
    )(*flat, gain_parts)


def heads_kernel(planes, groups, tpos, cpos, lens, x_ref, *refs):
    w_refs = refs[: planes * groups]
    terms_ref, out_ref, xbuf, wbuf, acc, qkv, sems_x, sems_w = refs[planes * groups :]
    rows_w = w_refs[0].shape[1]
    n = w_refs[0].shape[2]
    tokens = xbuf.shape[1]
    per = tokens // groups
    heads = n // DH

    def x_copies(p):
        return [
            pltpu.make_async_copy(
                x_ref.at[tpos[p], u], xbuf.at[p, pl.ds(u * per, per)], sems_x.at[p, u]
            )
            for u in range(groups)
        ]

    def w_copies(p):
        return [
            pltpu.make_async_copy(
                w_refs[p * groups + u],
                wbuf.at[p, :, pl.ds(pl.multiple_of(cpos[u] * rows_w, rows_w), rows_w)],
                sems_w.at[p, u],
            )
            for u in range(groups)
        ]

    for p in range(planes):
        for c in x_copies(p) + w_copies(p):
            c.start()

    block = min(tokens, 256)
    for p in range(planes):
        for c in x_copies(p) + w_copies(p):
            c.wait()

        @pl.loop(0, tokens // block)
        def _(i):
            rows = pl.ds(pl.multiple_of(i * block, block), block)
            x = xbuf[p, rows, :]
            for m in range(3):
                part = jnp.dot(x, wbuf[p, m], preferred_element_type=jnp.float32)
                if p > 0:
                    part = acc[m, rows, :] + part
                if p < planes - 1:
                    acc[m, rows, :] = part
                else:
                    qkv[m, rows, :] = part.astype(jnp.bfloat16)

    lane_head = lax.broadcasted_iota(jnp.int32, (LEN, n), 1) // DH
    key_pos = lax.broadcasted_iota(jnp.int32, (LEN, LEN), 1)

    @pl.loop(0, tokens // LEN)
    def _(i):
        rows = pl.ds(pl.multiple_of(i * LEN, LEN), LEN)
        q = qkv[0, rows, :]
        k = qkv[1, rows, :]
        v = qkv[2, rows, :]
        zero = jnp.zeros_like(k)
        live = key_pos < lens[i]
        total = None
        for h in range(heads):
            own = lane_head == h
            s = lax.dot_general(
                q, jnp.where(own, k, zero), (((1,), (1,)), ((), ())),
                preferred_element_type=jnp.float32,
            )
            s = jnp.where(live, s + terms_ref[h], -1e30)
            e = jnp.exp(s - jnp.max(s, axis=-1, keepdims=True))
            w = (e / jnp.sum(e, axis=-1, keepdims=True)).astype(jnp.bfloat16)
            o = jnp.dot(w, jnp.where(own, v, zero), preferred_element_type=jnp.float32)
            total = o if total is None else total + o
        out_ref[rows, :] = total.astype(jnp.bfloat16)


def heads_call(planes, groups, tpos, cpos, lens, normed, weights, terms):
    _, rows_w, n = weights[0].shape
    _, _, per, f = normed.shape
    tokens = groups * per
    return pl.pallas_call(
        functools.partial(heads_kernel, planes, groups),
        in_specs=[SMEM, SMEM, SMEM, ANY] + [ANY] * len(weights) + [VMEM],
        out_specs=VMEM,
        out_shape=jax.ShapeDtypeStruct((tokens, n), jnp.bfloat16),
        scratch_shapes=[
            pltpu.VMEM((planes, tokens, f), jnp.bfloat16),
            pltpu.VMEM((planes, 3, f, n), jnp.bfloat16),
            pltpu.VMEM((3, tokens, n), jnp.float32),
            pltpu.VMEM((3, tokens, n), jnp.bfloat16),
            pltpu.SemaphoreType.DMA((planes, groups)),
            pltpu.SemaphoreType.DMA((planes, groups)),
        ],
        compiler_params=pltpu.CompilerParams(vmem_limit_bytes=56 * 2**20),
        cost_estimate=pl.CostEstimate(
            flops=2 * tokens * planes * f * 3 * n,
            bytes_accessed=2 * planes * f * (tokens + 3 * n),
            transcendentals=tokens * LEN * n // DH,
        ),
        name="heads",
    )(tpos, cpos, lens, normed, *weights, terms)


def project_kernel(planes, groups, column, last, ppos, qpos, cpos, *refs):
    count = planes * groups
    a_refs, w_refs, refs = refs[:count], refs[count : 2 * count], refs[2 * count :]
    if last:
        add_ref, res_ref, out_ref, abuf, wbuf, total, sems_a, sems_w = refs
    else:
        out_ref, abuf, wbuf, total, sems_a, sems_w = refs
    _, part_rows, inner = w_refs[0].shape
    nc = a_refs[0].shape[1]
    per_group = inner // groups

    def copies(t):
        out = []
        for u in range(groups):
            spot = pl.multiple_of(cpos[u] * nc, nc)
            out.append(
                pltpu.make_async_copy(
                    a_refs[t * groups + u], abuf.at[t, :, pl.ds(spot, nc)], sems_a.at[t, u]
                )
            )
            for p in range(planes):
                row = pl.multiple_of((cpos[u] * planes + qpos[p]) * part_rows, part_rows)
                for c in range(groups):
                    out.append(
                        pltpu.make_async_copy(
                            w_refs[p * groups + u].at[
                                ppos[t * planes + p], :, pl.ds(c * per_group + column, nc)
                            ],
                            wbuf.at[t, pl.ds(row, part_rows), pl.ds(c * nc, nc)],
                            sems_w.at[t, p, u, c],
                        )
                    )
        return out

    for t in range(planes):
        for copy in copies(t):
            copy.start()

    rows = out_ref.shape[0]
    block = min(rows, 128)
    for t in range(planes):
        for copy in copies(t):
            copy.wait()

        @pl.loop(0, rows // block)
        def _(i):
            here = pl.ds(pl.multiple_of(i * block, block), block)
            part = lax.dot_general(
                abuf[t, here, :],
                wbuf[t],
                (((1,), (1,)), ((), ())),
                preferred_element_type=jnp.float32,
            )
            if t > 0:
                part = part + total[here, :]
            elif last:
                part = part + add_ref[here, :]
            if t < planes - 1:
                total[here, :] = part
            elif last:
                residual = res_ref[here, :].astype(jnp.float32)
                out_ref[here, :] = (residual + part).astype(jnp.bfloat16)
            else:
                out_ref[here, :] = part


def project_call(planes, groups, column, places, attended, weights, before=None, residual=None):
    last = residual is not None
    rows, nc = attended[0].shape
    _, part_rows, _ = weights[0].shape
    width = planes * groups * part_rows
    ends = [before, residual] if last else []
    return pl.pallas_call(
        functools.partial(project_kernel, planes, groups, column, last),
        in_specs=[SMEM] * 3 + [ANY] * (2 * planes * groups) + [VMEM] * len(ends),
        out_specs=VMEM,
        out_shape=jax.ShapeDtypeStruct((rows, width), jnp.bfloat16 if last else jnp.float32),
        scratch_shapes=[
            pltpu.VMEM((planes, rows, groups * nc), jnp.bfloat16),
            pltpu.VMEM((planes, width, groups * nc), jnp.bfloat16),
            pltpu.VMEM((rows, width), jnp.float32),
            pltpu.SemaphoreType.DMA((planes, groups)),
            pltpu.SemaphoreType.DMA((planes, planes, groups, groups)),
        ],
        compiler_params=pltpu.CompilerParams(vmem_limit_bytes=40 * 2**20),
        cost_estimate=pl.CostEstimate(
            flops=2 * rows * width * planes * groups * nc,
            bytes_accessed=2 * planes * groups * nc * (rows + width),
            transcendentals=0,
        ),
        name="project",
    )(*places, *attended, *weights, *ends)


def after(value, *others):
    return lax.optimization_barrier((value,) + others)[0]


def local(
    dp_size, mp_size, hidden, norm_gain, query_weight, keyvalue_weight, output_weight, position_bias, lengths
):
    planes = mp_size
    groups = dp_size // mp_size
    tokens, f = hidden.shape
    inner_here = query_weight.shape[2]
    n = inner_here // groups
    chunks = 2 if n // 2 % LANES == 0 else 1
    nc = n // chunks
    heads = nc // DH
    rows_w = query_weight.shape[1]
    device = lax.axis_index("dp")
    z = lax.axis_index("mp")
    k, c = device // groups, device % groups

    def dp_xor(x, m):
        return lax.ppermute(x, "dp", [(i, i ^ m) for i in range(dp_size)])

    def mp_xor(x, m):
        return lax.ppermute(x, "mp", [(i, i ^ m) for i in range(mp_size)])

    def over_mp(x):
        got = [x]
        for t in range(1, planes):
            source = x if is_power(t) else got[t ^ low_bit(t)]
            got.append(mp_xor(source, t if is_power(t) else low_bit(t)))
        return got

    p_range = jnp.arange(planes, dtype=jnp.int32)
    cpos = (c ^ jnp.arange(groups, dtype=jnp.int32)).astype(jnp.int32)
    tpos = (z ^ k ^ p_range).astype(jnp.int32)
    qpos = (k ^ p_range).astype(jnp.int32)
    ppos = (z ^ k ^ p_range[:, None] ^ p_range[None, :]).astype(jnp.int32).reshape(-1)

    with jax.named_scope("hidden"):
        pieces = over_mp(hidden)
        rows_of = [pieces]
        for u in range(1, groups):
            rows_of.append([dp_xor(piece, u) for piece in pieces])
    gain_parts = norm_gain[0].reshape(planes, f)[z ^ p_range]

    def payload(u, chunk):
        start = (c ^ u) * n + chunk * nc
        q = lax.dynamic_slice(query_weight[0], (0, start), (rows_w, nc))
        kv = lax.dynamic_slice(keyvalue_weight[0], (0, 0, start), (rows_w, 2, nc))
        return jnp.stack([q, kv[:, 0], kv[:, 1]])

    chunk_weights = []
    tie = ()
    for chunk in range(chunks):
        with jax.named_scope("weights%d" % chunk):
            got = {}
            for u in range(groups):
                own = after(payload(u, chunk), *tie)
                for p in range(planes):
                    if p == 0:
                        got[p, u] = own if u == 0 else dp_xor(own, u)
                    elif is_power(p):
                        got[p, u] = dp_xor(own, p * groups ^ u)
            tie = tuple(got[p, u] for u in range(groups) for p in range(1, planes) if is_power(p))
            for u in range(groups):
                for p in range(1, planes):
                    if not is_power(p):
                        b = low_bit(p) if u % 2 == 0 else high_bit(p)
                        got[p, u] = dp_xor(got[p ^ b, u], b * groups)
            chunk_weights.append([got[p, u] for p in range(planes) for u in range(groups)])

    with jax.named_scope("turn"):
        part = rows_w // planes
        source = after(output_weight[0], *pieces[1:])
        moved = []
        for p in range(planes):
            block = lax.dynamic_slice(source, ((z ^ p) * part, 0), (part, inner_here))
            pairs = []
            for kk in range(planes):
                for cc in range(groups):
                    for zz in range(planes):
                        target = (zz ^ p) * groups + cc
                        pairs.append(((kk * groups + cc) * mp_size + zz, target * mp_size + kk))
            moved.append(lax.ppermute(block, ("dp", "mp"), pairs))
        turned = jnp.stack(moved)
    with jax.named_scope("output_weights"):
        turned = after(turned, *tie)
        out_got = {(0, 0): turned}
        for p in range(1, planes):
            if is_power(p):
                out_got[p, 0] = dp_xor(turned, p * groups)
        middle = planes // 2
        for p in range(1, planes):
            if not is_power(p):
                lo = dp_xor(out_got[p ^ low_bit(p), 0][:middle], low_bit(p) * groups)
                hi = dp_xor(out_got[p ^ high_bit(p), 0][middle:], high_bit(p) * groups)
                out_got[p, 0] = jnp.concatenate([lo, hi])
        for u in range(1, groups):
            for p in range(planes):
                out_got[p, u] = dp_xor(out_got[p, 0], u)
        out_weights = [out_got[p, u] for p in range(planes) for u in range(groups)]

    bucket_onehot = jnp.asarray(
        (bucket_table()[:, :, None] == np.arange(BUCKETS)[None, None, :]).astype(np.float32)
    )
    own_bias = lax.dynamic_slice(
        position_bias[0], (0, c * (n // DH)), (BUCKETS, n // DH)
    )
    terms = jnp.einsum("qkb,bh->hqk", bucket_onehot, own_bias, precision=lax.Precision.HIGHEST)
    lens = jnp.concatenate([lengths] + [dp_xor(lengths, u) for u in range(1, groups)])

    normed = norm_call(rows_of, gain_parts)

    total = None
    for chunk in range(chunks):
        attended = heads_call(
            planes,
            groups,
            tpos,
            cpos,
            lens,
            normed,
            chunk_weights[chunk],
            terms[chunk * heads : (chunk + 1) * heads],
        )
        with jax.named_scope("attended%d" % chunk):
            blocks = []
            for u in range(groups):
                block = attended[u * tokens : (u + 1) * tokens]
                blocks.append(over_mp(block if u == 0 else dp_xor(block, u)))
        flat = [blocks[u][t] for t in range(planes) for u in range(groups)]
        if chunk < chunks - 1:
            ends = {}
            assert chunks == 2
        else:
            ends = {"before": total, "residual": hidden}
            if total is None:
                ends["before"] = jnp.zeros((tokens, f), jnp.float32)
        total = project_call(
            planes, groups, chunk * nc, (ppos, qpos, cpos), flat, out_weights, **ends
        )
    return total


def solution(mesh):
    in_specs = (
        P("dp", "mp"),
        P(),
        P(None, "dp", "mp"),
        P(None, "dp", None, "mp"),
        P(None, "dp", "mp"),
        P(None, None, "mp"),
        P("dp"),
    )
    out_specs = P("dp", "mp")
    body = functools.partial(local, mesh.shape["dp"], mesh.shape["mp"])
    return jax.shard_map(body, mesh=mesh, in_specs=in_specs, out_specs=out_specs, check_vma=False)
```
